256 devices in a mesh: expert: 8 (over y, core), dp: 32 (over x, z).
Axes of the slice: x: 4, y: 4, z: 8, core: 2. Of those that a mesh axis runs over, the one named last changes fastest.
Arguments:
- tokens: bfloat16 [32768, 4096], P(('expert', 'dp')), may hold values from -6 to 6
- gates: float32 [32768, 8], P(('expert', 'dp')), may hold values from 0.05 to 1
- routes: int32 [32768, 8], P(('expert', 'dp')), may hold values from 0 to 127, all different within a row; in each aligned block of 128 rows (0 to 127, 128 to 255, ...) at most 16 rows name the same one
- doc_ids: int32 [32768], P(('expert', 'dp')), may hold values from 0 to 1
- hidden_grad: bfloat16 [128, 4096, 1536], P('expert', 'dp'), may hold values from -6 to 6
- proj_in: bfloat16 [4096, 64], replicated, may hold values from -0.09375 to 0.09375
- proj_out: bfloat16 [128, 1536, 64], P('expert'), may hold values from -0.15625 to 0.15625
- val_features: bfloat16 [128, 128, 4096], P('dp', 'expert'), may hold values from -6 to 6
Outputs:
- scores: float32 [64, 128], P('dp')
The draws below stay inside these ranges and needn't reach their ends.
Inputs may be any that keep to these rules, and one draw needn't show every extreme that they name: Each row names 8 different experts; among the rows of one device no expert is named by more than 16 routes, and in every draw some expert by exactly 16.
All inputs are finite; a program needn't handle non-finite values.
Results may differ from the reference program's by a relative error of at most 0.0049.
Values may be sent and summed in bfloat16 or wider, within the bound.
A program may use at most 64 MiB of HBM per device.

```python
import math
import jax
import jax.numpy as jnp
import numpy as np
from jax import lax

D = 4096
FF = 1536
EXPERTS = 128
TOPK = 8
RANK = 64
TOK_DEV = 128
CAP = 16
DOC_GRP = 2
VAL = 128
N_EXPERT = 8
N_DP = 32


def set_ends(entries, own_key, low, largest):
    longest = entries.shape.index(max(entries.shape))
    spots = []
    for shift in (0, 1):
        where = [jax.random.randint(jax.random.fold_in(own_key, axis), (), 0, length) for axis, length in enumerate(entries.shape)]
        where[longest] = (where[longest] + shift) % entries.shape[longest]
        spots.append(tuple(where))
    return entries.at[spots[0]].set(low).at[spots[1]].set(largest)


def level_of(rng, extent, split, smallest, top_value):
    def one(dim, blocks):
        draws = jax.random.uniform(jax.random.fold_in(jax.random.fold_in(rng, 6), dim), (blocks,), jnp.float32, smallest / len(split), top_value / len(split))
        return jnp.repeat(jnp.exp(draws), extent[dim] // blocks).reshape((-1,) + (1,) * (len(extent) - dim - 1))

    level = one(*split[0])
    for cut in split[1:]:
        level = level * one(*cut)
    return level


def shared_out(stream_key, own, number, rows, number_of, top, reach, slope):
    sequence = jax.random.permutation(stream_key, number_of)
    crowded, usual = load_shares(number_of, rows * top, reach, slope, True), load_shares(number_of, rows * top, reach, slope, False)
    places = jnp.arange(number_of)

    def named(tallies, rotation):
        used = int((tallies > 0).sum())
        fixed = max(1, used // 4)
        passed = fixed + (places - fixed + rotation * (used - fixed)) % max(1, number_of - fixed)
        return jnp.zeros((number_of,), jnp.int32).at[sequence[jnp.where(places < fixed, places, passed)]].set(jnp.asarray(tallies, jnp.int32))

    tallies = jnp.where(number % 4 == 0, named(crowded, number // 4), named(usual, number - number // 4 - 1))
    mixed = jax.random.permutation(jax.random.fold_in(own, 3), number_of)
    giver, taker = mixed[0:number_of // 2 * 2:2], mixed[1:number_of // 2 * 2:2]
    slack = jnp.minimum(tallies[giver] - 1, reach - tallies[taker]) // 2
    slack = jnp.where((giver == sequence[0]) | (taker == sequence[0]) | (tallies[taker] == 0), 0, jnp.maximum(slack, 0))
    passed = jax.random.randint(jax.random.fold_in(own, 4), (number_of // 2,), 0, 1 << 20) % (slack + 1)
    tallies = tallies.at[giver].add(-passed).at[taker].add(passed)
    labels = jnp.searchsorted(jnp.cumsum(tallies), jnp.arange(rows * top), side="right").astype(jnp.int32)
    table = labels.reshape(top, rows).T
    table = table[jax.random.permutation(jax.random.fold_in(own, 1), rows)]
    rotation = jax.random.randint(jax.random.fold_in(own, 2), (rows, 1), 0, top)
    return jnp.take_along_axis(table, (jnp.arange(top)[None, :] + rotation) % top, axis=1)


def load_shares(amount, total, bound, lean, full):
    portions = [(1 << 20) // math.isqrt(grade ** lean) + 1 for grade in range(1, amount + 1)]
    largest = bound if full else min(bound, max(-(-total // amount), total * portions[0] // sum(portions)))
    least = 1 if total - largest >= amount - 1 else 0
    holding, rest = [largest] + [least] * (amount - 1), total - largest - least * (amount - 1)
    while rest > 0:
        movable = [i for i in range(1, amount) if holding[i] < largest] or [i for i in range(1, amount) if holding[i] < bound]
        mass, budget = sum([portions[i] for i in movable]), rest
        for i in movable:
            extra = min(bound - holding[i], max(1, budget * portions[i] // mass), rest)
            holding[i] = holding[i] + extra
            rest = rest - extra
    return np.array(holding)


def gaussian(key, extent, scale, bound, cuts=(), kind=jnp.bfloat16):
    values = scale * jax.random.normal(key, extent, jnp.float32)
    if cuts:
        values = values * level_of(key, extent, cuts, -0.22, 0.18)
    return jnp.clip(values, -bound, bound).astype(kind)


def setup_inputs(seed: int = 0) -> dict:
    keys = jax.random.split(jax.random.key(seed), 9)
    tokens = gaussian(keys[0], (N_EXPERT * N_DP * TOK_DEV, D), 1.0, 6.0, ((0, 256),))
    gates = jnp.clip(jnp.exp(math.log(1.0) - 2.9957323 * jax.random.uniform(keys[1], (N_EXPERT * N_DP * TOK_DEV, TOPK), jnp.float32) ** level_of(keys[1], (N_EXPERT * N_DP * TOK_DEV, TOPK), ((0, 256),), -0.2, 0.2)), 0.05, 1.0)
    routes_keys = jax.random.split(jax.random.fold_in(keys[2], 1), (N_EXPERT * N_DP * TOK_DEV) // TOK_DEV)
    routes_turns = jax.random.permutation(jax.random.fold_in(keys[2], 3), (N_EXPERT * N_DP * TOK_DEV) // TOK_DEV)
    routes = jax.vmap(lambda own, number: shared_out(jax.random.fold_in(keys[2], 2), own, number, TOK_DEV, EXPERTS, TOPK, CAP, 2))(routes_keys, routes_turns).reshape((N_EXPERT * N_DP * TOK_DEV, TOPK))
    doc_ids = set_ends(jax.random.randint(keys[3], (N_EXPERT * N_DP * TOK_DEV,), 0, DOC_GRP), jax.random.fold_in(keys[3], 1), 0, DOC_GRP - 1).astype(jnp.int32)
    hidden_grad = gaussian(keys[4], (EXPERTS, N_DP * N_EXPERT * CAP, FF), 1.0, 6.0, ((0, 8), (1, 32)))
    proj_in = gaussian(keys[5], (D, RANK), D ** -0.5, 0.09375)
    proj_out = gaussian(keys[6], (EXPERTS, FF, RANK), FF ** -0.5, 0.15625, ((0, 8),))
    val_features = gaussian(keys[7], (VAL, EXPERTS, RANK * RANK), 1.0, 6.0, ((0, 32), (1, 8)))
    return dict(tokens=tokens, gates=gates, routes=routes, doc_ids=doc_ids, hidden_grad=hidden_grad, proj_in=proj_in, proj_out=proj_out, val_features=val_features)


def slot_of(block):
    onehot = (block[:, None] == jnp.arange(EXPERTS, dtype=jnp.int32)[None, :]).astype(jnp.int32)
    prior = jnp.cumsum(onehot, axis=0) - onehot
    return lax.optimization_barrier(jnp.sum(prior * onehot, axis=1)).astype(jnp.int32)

def expert_features(items):
    grad_rows, proj_rows, acts, owners = items
    lowered = jnp.dot(grad_rows, proj_rows, preferred_element_type=jnp.float32).astype(jnp.bfloat16)
    member = (owners[:, None] == jnp.arange(DOC_GRP, dtype=jnp.int32)[None, :]).astype(jnp.float32)
    member = member.reshape(N_DP, N_EXPERT * CAP, DOC_GRP)
    left = acts.astype(jnp.float32).reshape(N_DP, N_EXPERT * CAP, RANK)
    right = lowered.astype(jnp.float32).reshape(N_DP, N_EXPERT * CAP, RANK)
    spread = (member[:, :, :, None] * left[:, :, None, :]).reshape(N_DP, N_EXPERT * CAP, DOC_GRP * RANK)
    feats = jnp.einsum('grm,grb->gmb', spread, right)
    return feats.reshape(N_DP, DOC_GRP, RANK * RANK).astype(jnp.bfloat16)

def reference(tokens, gates, routes, doc_ids, hidden_grad, proj_in, proj_out, val_features):
    total = tokens.shape[0]
    rows = N_DP * N_EXPERT * CAP
    act = jnp.dot(tokens, proj_in, preferred_element_type=jnp.float32)
    sent = (gates[:, :, None] * act[:, None, :]).astype(jnp.bfloat16)
    slots = lax.map(slot_of, routes.reshape(N_EXPERT * N_DP, TOK_DEV * TOPK)).reshape(total, TOPK)
    device = jnp.arange(total, dtype=jnp.int32) // TOK_DEV
    source = device // N_DP
    group = device % N_DP
    row = group[:, None] * (N_EXPERT * CAP) + source[:, None] * CAP + slots
    index = (routes * rows + row).reshape(-1).astype(jnp.int32)
    filled = jnp.zeros((EXPERTS * rows, RANK), jnp.bfloat16).at[index].set(sent.reshape(-1, RANK))
    owner_ids = jnp.full((EXPERTS * rows,), DOC_GRP, jnp.int32).at[index].set(jnp.repeat(doc_ids, TOPK).astype(jnp.int32))
    feats = lax.map(expert_features, (hidden_grad, proj_out, filled.reshape(EXPERTS, rows, RANK), owner_ids.reshape(EXPERTS, rows)))
    flat = jnp.transpose(feats, (1, 2, 0, 3)).reshape(N_DP * DOC_GRP, EXPERTS * RANK * RANK)
    vals = val_features.reshape(val_features.shape[0], EXPERTS * RANK * RANK)
    total_scores = lax.dot_general(flat, vals, (((1,), (1,)), ((), ())), preferred_element_type=jnp.float32)
    return total_scores / jnp.sqrt(jnp.float32(EXPERTS * RANK * RANK))
```

```python
import functools

import jax
import jax.numpy as jnp
from jax import lax
from jax.experimental import pallas as pl
from jax.experimental.pallas import tpu as pltpu
from jax.sharding import PartitionSpec as P

MESH = pl.DeviceIdType.MESH
BF = jnp.bfloat16
F32 = jnp.float32
NT = (((1,), (1,)), ((), ()))


def iota(shape, dim):
    return lax.broadcasted_iota(jnp.int32, shape, dim)


def dot(a, b):
    return jnp.dot(a, b, preferred_element_type=F32)


def dot_nt(a, b):
    return lax.dot_general(a, b, NT, preferred_element_type=F32)


def whole(ref, sem):
    pltpu.make_async_copy(ref, ref, sem).wait()


def kernel(
    n_dp, n_ex,
    tok_hbm, gate_hbm, route_hbm, doc_hbm, grad_hbm, pin_hbm, pout_hbm, val_hbm,
    out_ref,
    tok, gate, route, doc, grad, pin, pout,
    slots, gated, ysend, yrecv, diag, feats, raw, vals, train, part, owned, total, mine,
    in_sem, pair_sem, val_s, val_r, act_s, act_r, train_s, train_r, part_s, part_r, own_s, own_r,
):
    me = lax.axis_index("dp")
    ex = lax.axis_index("expert")

    def dp_at(k):
        return lax.rem(me + k, n_dp)

    def ex_at(k):
        return lax.rem(ex + k, n_ex)

    loads = [
        pltpu.make_async_copy(src, dst, in_sem.at[n])
        for n, (src, dst) in enumerate(
            [(route_hbm, route), (gate_hbm, gate), (doc_hbm, doc), (pin_hbm, pin), (tok_hbm, tok)]
        )
    ]
    for load in loads:
        load.start()

    def pair_loads(c):
        rows, cols = pl.ds(pl.multiple_of(c * 256, 256), 256), pl.ds(pl.multiple_of(c * 128, 128), 128)
        return (
            pltpu.make_async_copy(grad_hbm.at[rows], grad.at[rows], pair_sem.at[0, c]),
            pltpu.make_async_copy(pout_hbm.at[cols], pout.at[cols], pair_sem.at[1, c]),
        )

    barrier = pltpu.get_barrier_semaphore()

    @pl.loop(1, n_dp)
    def _(k):
        pl.semaphore_signal(barrier, inc=1, device_id=(ex, dp_at(k)), device_id_type=MESH)

    @pl.loop(1, n_ex)
    def _(k):
        pl.semaphore_signal(barrier, inc=1, device_id=(ex_at(k), me), device_id_type=MESH)

    @pl.loop(0, 8)
    def _(c):
        for load in pair_loads(c):
            load.start()

    for load in loads[:3]:
        load.wait()
    experts = iota((128, 128), 0)
    named = jnp.zeros((128, 128), F32)
    weight = jnp.zeros((128, 128), F32)
    for k in range(8):
        hit = route[k : k + 1, :] == experts
        named = jnp.where(hit, 1.0, named)
        weight = jnp.where(hit, gate[k : k + 1, :], weight)
    earlier = (iota((128, 128), 0) < iota((128, 128), 1)).astype(BF)
    slots[...] = jnp.where(named > 0.0, dot(named.astype(BF), earlier), -1.0)
    gated[...] = weight

    @pl.loop(0, 16)
    def _(r):
        diag[:, pl.ds(pl.multiple_of(r * 64, 64), 64), :] = jnp.zeros((2, 64, 512), BF)

    for load in loads[3:]:
        load.wait()
    act = dot_nt(pin[...], tok[...])
    act_hi = act.astype(BF)
    act_lo = (act - act_hi.astype(F32)).astype(BF)
    row, col = iota((128, 64), 0), iota((128, 64), 1)
    spread = (col == 2 * ((row % 64) // 2) + row // 64).astype(BF)
    member = iota((128, 128), 0) % 2 == doc[...]
    x_hi = jnp.where(member, dot(spread, act_hi), 0.0).astype(BF)
    x_lo = jnp.where(member, dot(spread, act_lo), 0.0).astype(BF)

    place = iota((16, 128), 0).astype(F32)

    @pl.loop(0, n_ex)
    def _(g):
        blocks = []
        for e in range(16):
            at = pl.ds(g * 16 + e, 1)
            blocks.append(jnp.where(slots[at, :] == place, gated[at, :], 0.0))
        pick = jnp.concatenate(blocks, axis=0)
        pick_hi = pick.astype(BF)
        pick_lo = (pick - pick_hi.astype(F32)).astype(BF)
        y = dot_nt(x_hi, pick_hi) + dot_nt(x_lo, pick_hi) + dot_nt(x_hi, pick_lo)
        y = y.astype(BF)
        ysend[g, 0] = y[:, :128]
        ysend[g, 1] = y[:, 128:]

    pl.semaphore_wait(barrier, n_dp - 1 + n_ex - 1)

    def act_dst():
        return yrecv.at[:, :, pl.ds(pl.multiple_of(ex * 128, 128), 128)]

    @pl.loop(1, n_ex)
    def _(k):
        to = ex_at(k)
        pltpu.make_async_remote_copy(
            ysend.at[to], act_dst(), act_s, act_r, device_id=(to, me), device_id_type=MESH
        ).start()

    pltpu.make_async_copy(ysend.at[ex], act_dst(), act_r).start()

    def val_src(to):
        return val_hbm.at[:, :, pl.ds(pl.multiple_of(to * 128, 128), 128)]

    def val_dst():
        return raw.at[pl.ds(me * 4, 4)]

    @pl.loop(1, n_dp)
    def _(k):
        to = dp_at(k)
        pltpu.make_async_remote_copy(
            val_src(to), val_dst(), val_s, val_r, device_id=(ex, to), device_id_type=MESH
        ).start()

    pltpu.make_async_copy(val_src(me), val_dst(), val_r).start()

    own_half = (iota((256, 128), 0) // 128) == (iota((256, 128), 1) // 64)

    @pl.loop(0, 8)
    def _(c):
        for load in pair_loads(c):
            load.wait()
        both = dot_nt(
            grad[pl.ds(pl.multiple_of(c * 256, 256), 256), :],
            pout[pl.ds(pl.multiple_of(c * 128, 128), 128), :],
        )
        both = jnp.where(own_half, both, 0.0).astype(BF)
        half, inner = c // 4, lax.rem(c, 4)
        cols = pl.ds(pl.multiple_of(inner * 128, 128), 128)
        for i in range(8):
            for e in range(2):
                rows = pl.ds(pl.multiple_of(i * 128 + inner * 32 + e * 16, 16), 16)
                diag[half, rows, cols] = both[e * 128 + i * 16 : e * 128 + i * 16 + 16, :]

    whole(yrecv, act_r)
    low = iota((64, 128), 1) < 64

    @pl.loop(0, 4)
    def _(q):
        half, inner = q // 2, lax.rem(q, 2)
        cols = pl.ds(pl.multiple_of(inner * 256, 256), 256)
        f = dot(yrecv[half], diag[half, :, cols])
        for h in range(2):
            even, odd = f[:64, h * 128 : h * 128 + 128], f[64:, h * 128 : h * 128 + 128]
            feats[4 * q + 2 * h] = jnp.where(low, even, pltpu.roll(odd, 64, 1)).astype(BF)
            feats[4 * q + 2 * h + 1] = jnp.where(low, pltpu.roll(even, 64, 1), odd).astype(BF)

    def pair(ref, at):
        return ref.at[:, pl.ds(at * 2, 2), :]

    @pl.loop(1, n_dp)
    def _(k):
        to = dp_at(k)
        pltpu.make_async_remote_copy(
            pair(feats, to), pair(train, me), train_s, train_r, device_id=(ex, to), device_id_type=MESH
        ).start()

    pltpu.make_async_copy(pair(feats, me), pair(train, me), train_r).start()

    row, col = iota((256, 256), 0), iota((256, 256), 1)
    swap = ((row // 16 == col % 16) & (row % 16 == col // 16)).astype(BF)
    whole(raw, val_r)

    @pl.loop(0, 8)
    def _(b):
        at = pl.ds(pl.multiple_of(b * 16, 16), 16)
        turned = dot(swap, raw[at].reshape(256, 128)).astype(BF)
        for e in range(16):
            vals[e, at, :] = turned[e * 16 : e * 16 + 16, :]

    whole(train, train_r)
    score = jnp.zeros((64, 128), F32)
    for e in range(16):
        score += dot_nt(train[e], vals[e])
    part[...] = score

    def two(ref, at):
        return ref.at[pl.ds(at * 2, 2), :]

    @pl.loop(1, n_dp)
    def _(k):
        to = dp_at(k)
        pltpu.make_async_remote_copy(
            two(part, to), two(owned, me), part_s, part_r, device_id=(ex, to), device_id_type=MESH
        ).start()

    pltpu.make_async_copy(two(part, me), two(owned, me), part_r).start()
    whole(owned, part_r)

    def folded(value):
        value = value + pltpu.roll(value, 4, 0)
        return value + pltpu.roll(value, 2, 0)

    rows = owned[0:8, :]
    for n in range(1, 8):
        rows += owned[8 * n : 8 * n + 8, :]
    mine[...] = folded(rows)

    @pl.loop(1, n_ex)
    def _(k):
        pltpu.make_async_remote_copy(
            mine.at[0:2, :], two(total, ex), own_s, own_r, device_id=(ex_at(k), me), device_id_type=MESH
        ).start()

    pltpu.make_async_copy(mine.at[0:2, :], two(total, ex), own_r).start()
    whole(total, own_r)
    out_ref[...] = folded(total[0:8, :] + total[8:16, :])[0:2, :]

    whole(yrecv.at[:, :, 0:896], act_s)
    whole(raw.at[0:124], val_s)
    whole(train.at[:, 0:62, :], train_s)
    whole(owned.at[0:62, :], part_s)
    whole(total.at[0:14, :], own_s)


def body(tokens, gates, routes, doc_ids, hidden_grad, proj_in, proj_out, val_features):
    n_dp, n_ex = lax.axis_size("dp"), lax.axis_size("expert")
    entries = proj_out.shape[0] * n_ex * proj_in.shape[1] ** 2
    dma = pltpu.SemaphoreType.DMA
    summed = pl.pallas_call(
        functools.partial(kernel, n_dp, n_ex),
        out_shape=jax.ShapeDtypeStruct((2, 128), F32),
        in_specs=[pl.BlockSpec(memory_space=pltpu.HBM)] * 8,
        out_specs=pl.BlockSpec(memory_space=pltpu.VMEM),
        scratch_shapes=[
            pltpu.VMEM((128, 4096), BF),
            pltpu.VMEM((8, 128), F32),
            pltpu.VMEM((8, 128), jnp.int32),
            pltpu.VMEM((1, 128), jnp.int32),
            pltpu.VMEM((2048, 1536), BF),
            pltpu.VMEM((64, 4096), BF),
            pltpu.VMEM((1024, 1536), BF),
            pltpu.VMEM((128, 128), F32),
            pltpu.VMEM((128, 128), F32),
            pltpu.VMEM((8, 2, 128, 128), BF),
            pltpu.VMEM((2, 128, 1024), BF),
            pltpu.VMEM((2, 1024, 512), BF),
            pltpu.VMEM((16, 64, 128), BF),
            pltpu.VMEM((128, 16, 128), BF),
            pltpu.VMEM((16, 128, 128), BF),
            pltpu.VMEM((16, 64, 128), BF),
            pltpu.VMEM((64, 128), F32),
            pltpu.VMEM((64, 128), F32),
            pltpu.VMEM((16, 128), F32),
            pltpu.VMEM((8, 128), F32),
            dma((5,)),
            dma((2, 8)),
        ]
        + [dma] * 10,
        compiler_params=pltpu.CompilerParams(
            collective_id=0, has_side_effects=True, vmem_limit_bytes=48 << 20
        ),
    )(
        tokens,
        gates.T,
        routes.T,
        doc_ids.reshape(1, -1),
        hidden_grad.reshape(-1, hidden_grad.shape[2]),
        proj_in.T,
        jnp.swapaxes(proj_out, 1, 2).reshape(-1, proj_out.shape[1]),
        val_features,
    )
    return summed * (1.0 / jnp.sqrt(F32(entries)))


def solution(mesh):
    in_specs = (
        P(("expert", "dp"), None),
        P(("expert", "dp"), None),
        P(("expert", "dp"), None),
        P(("expert", "dp")),
        P("expert", "dp", None),
        P(),
        P("expert", None, None),
        P("dp", "expert", None),
    )
    return jax.shard_map(body, mesh=mesh, in_specs=in_specs, out_specs=P("dp", None), check_vma=False)
```

```python
import functools

import jax
import jax.numpy as jnp
from jax import lax
from jax.experimental import pallas as pl
from jax.experimental.pallas import tpu as pltpu
from jax.sharding import PartitionSpec as P

MESH = pl.DeviceIdType.MESH
BF = jnp.bfloat16
F32 = jnp.float32
NT = (((1,), (1,)), ((), ()))
RING_Z = 8


def iota(shape, dim):
    return lax.broadcasted_iota(jnp.int32, shape, dim)


def dot(a, b):
    return jnp.dot(a, b, preferred_element_type=F32)


def dot_nt(a, b):
    return lax.dot_general(a, b, NT, preferred_element_type=F32)


def whole(ref, sem):
    pltpu.make_async_copy(ref, ref, sem).wait()


def kernel(
    n_dp, n_ex,
    tok_hbm, gate_hbm, route_hbm, doc_hbm, grad_hbm, pin_hbm, pout_hbm, val_hbm,
    out_ref,
    tok, gate, route, doc, grad, pin, pout,
    slots, gated, ysend, yrecv, diag, feats, raw, vals, train, part, owned, total, mine,
    in_sem, pair_sem, val_s, val_r, act_s, act_r, train_s, train_r, part_s, part_r, own_s, own_r,
):
    me = lax.axis_index("dp")
    ex = lax.axis_index("expert")

    def outward(k, n):
        return n // 2 + jnp.where(lax.rem(k, 2) == 0, k // 2, -((k + 1) // 2))

    def dp_at(k):
        x, z = me // RING_Z, lax.rem(me, RING_Z)
        x = lax.rem(x + outward(k // RING_Z, n_dp // RING_Z), n_dp // RING_Z)
        z = lax.rem(z + outward(lax.rem(k, RING_Z), RING_Z), RING_Z)
        return x * RING_Z + z

    def ex_at(k):
        return lax.rem(ex + k, n_ex)

    barrier = pltpu.get_barrier_semaphore()

    @pl.loop(0, n_dp - 1)
    def _(k):
        pl.semaphore_signal(barrier, inc=1, device_id=(ex, dp_at(k)), device_id_type=MESH)

    @pl.loop(1, n_ex)
    def _(k):
        pl.semaphore_signal(barrier, inc=1, device_id=(ex_at(k), me), device_id_type=MESH)

    loads = [
        pltpu.make_async_copy(src, dst, in_sem.at[n])
        for n, (src, dst) in enumerate(
            [(route_hbm, route), (gate_hbm, gate), (doc_hbm, doc), (pin_hbm, pin), (tok_hbm, tok)]
        )
    ]
    for load in loads:
        load.start()

    def pair_loads(c):
        rows, cols = pl.ds(pl.multiple_of(c * 256, 256), 256), pl.ds(pl.multiple_of(c * 128, 128), 128)
        return (
            pltpu.make_async_copy(grad_hbm.at[rows], grad.at[rows], pair_sem.at[0, c]),
            pltpu.make_async_copy(pout_hbm.at[cols], pout.at[cols], pair_sem.at[1, c]),
        )

    @pl.loop(0, 8)
    def _(c):
        for load in pair_loads(c):
            load.start()

    for load in loads[:3]:
        load.wait()
    experts = iota((128, 128), 0)
    named = jnp.zeros((128, 128), F32)
    weight = jnp.zeros((128, 128), F32)
    for k in range(8):
        hit = route[k : k + 1, :] == experts
        named = jnp.where(hit, 1.0, named)
        weight = jnp.where(hit, gate[k : k + 1, :], weight)
    earlier = (iota((128, 128), 0) < iota((128, 128), 1)).astype(BF)
    slots[...] = jnp.where(named > 0.0, dot(named.astype(BF), earlier), -1.0)
    gated[...] = weight

    @pl.loop(0, 16)
    def _(r):
        diag[:, pl.ds(pl.multiple_of(r * 64, 64), 64), :] = jnp.zeros((2, 64, 512), BF)

    for load in loads[3:]:
        load.wait()
    act = dot_nt(pin[...], tok[...])
    act_hi = act.astype(BF)
    act_lo = (act - act_hi.astype(F32)).astype(BF)
    row, col = iota((128, 64), 0), iota((128, 64), 1)
    spread = (col == 2 * ((row % 64) // 2) + row // 64).astype(BF)
    member = iota((128, 128), 0) % 2 == doc[...]
    x_hi = jnp.where(member, dot(spread, act_hi), 0.0).astype(BF)
    x_lo = jnp.where(member, dot(spread, act_lo), 0.0).astype(BF)

    place = iota((16, 128), 0).astype(F32)

    @pl.loop(0, n_ex)
    def _(g):
        blocks = []
        for e in range(16):
            at = pl.ds(g * 16 + e, 1)
            blocks.append(jnp.where(slots[at, :] == place, gated[at, :], 0.0))
        pick = jnp.concatenate(blocks, axis=0)
        pick_hi = pick.astype(BF)
        pick_lo = (pick - pick_hi.astype(F32)).astype(BF)
        y = dot_nt(x_hi, pick_hi) + dot_nt(x_lo, pick_hi) + dot_nt(x_hi, pick_lo)
        y = y.astype(BF)
        ysend[g, 0] = y[:, :128]
        ysend[g, 1] = y[:, 128:]

    pl.semaphore_wait(barrier, n_dp - 1 + n_ex - 1)

    def act_dst():
        return yrecv.at[:, :, pl.ds(pl.multiple_of(ex * 128, 128), 128)]

    @pl.loop(1, n_ex)
    def _(k):
        to = ex_at(k)
        pltpu.make_async_remote_copy(
            ysend.at[to], act_dst(), act_s, act_r, device_id=(to, me), device_id_type=MESH
        ).start()

    pltpu.make_async_copy(ysend.at[ex], act_dst(), act_r).start()

    def val_src(to):
        return val_hbm.at[:, :, pl.ds(pl.multiple_of(to * 128, 128), 128)]

    def val_dst():
        return raw.at[pl.ds(me * 4, 4)]

    @pl.loop(0, n_dp - 1)
    def _(k):
        to = dp_at(k)
        pltpu.make_async_remote_copy(
            val_src(to), val_dst(), val_s, val_r, device_id=(ex, to), device_id_type=MESH
        ).start()

    pltpu.make_async_copy(val_src(me), val_dst(), val_r).start()

    own_half = (iota((256, 128), 0) // 128) == (iota((256, 128), 1) // 64)

    @pl.loop(0, 8)
    def _(c):
        for load in pair_loads(c):
            load.wait()
        both = dot_nt(
            grad[pl.ds(pl.multiple_of(c * 256, 256), 256), :],
            pout[pl.ds(pl.multiple_of(c * 128, 128), 128), :],
        )
        both = jnp.where(own_half, both, 0.0).astype(BF)
        half, inner = c // 4, lax.rem(c, 4)
        cols = pl.ds(pl.multiple_of(inner * 128, 128), 128)
        for i in range(8):
            for e in range(2):
                rows = pl.ds(pl.multiple_of(i * 128 + inner * 32 + e * 16, 16), 16)
                diag[half, rows, cols] = both[e * 128 + i * 16 : e * 128 + i * 16 + 16, :]

    whole(yrecv, act_r)
    low = iota((64, 128), 1) < 64

    @pl.loop(0, 4)
    def _(q):
        half, inner = q // 2, lax.rem(q, 2)
        cols = pl.ds(pl.multiple_of(inner * 256, 256), 256)
        f = dot(yrecv[half], diag[half, :, cols])
        for h in range(2):
            even, odd = f[:64, h * 128 : h * 128 + 128], f[64:, h * 128 : h * 128 + 128]
            feats[4 * q + 2 * h] = jnp.where(low, even, pltpu.roll(odd, 64, 1)).astype(BF)
            feats[4 * q + 2 * h + 1] = jnp.where(low, pltpu.roll(even, 64, 1), odd).astype(BF)

    def pair(ref, at):
        return ref.at[:, pl.ds(at * 2, 2), :]

    @pl.loop(0, n_dp - 1)
    def _(k):
        to = dp_at(k)
        pltpu.make_async_remote_copy(
            pair(feats, to), pair(train, me), train_s, train_r, device_id=(ex, to), device_id_type=MESH
        ).start()

    pltpu.make_async_copy(pair(feats, me), pair(train, me), train_r).start()

    row, col = iota((256, 256), 0), iota((256, 256), 1)
    swap = ((row // 16 == col % 16) & (row % 16 == col // 16)).astype(BF)
    whole(raw, val_r)

    @pl.loop(0, 8)
    def _(b):
        at = pl.ds(pl.multiple_of(b * 16, 16), 16)
        turned = dot(swap, raw[at].reshape(256, 128)).astype(BF)
        for e in range(16):
            vals[e, at, :] = turned[e * 16 : e * 16 + 16, :]

    whole(train, train_r)
    score = jnp.zeros((64, 128), F32)
    for e in range(16):
        score += dot_nt(train[e], vals[e])
    part[...] = score

    def two(ref, at):
        return ref.at[pl.ds(at * 2, 2), :]

    @pl.loop(0, n_dp - 1)
    def _(k):
        to = dp_at(k)
        pltpu.make_async_remote_copy(
            two(part, to), two(owned, me), part_s, part_r, device_id=(ex, to), device_id_type=MESH
        ).start()

    pltpu.make_async_copy(two(part, me), two(owned, me), part_r).start()
    whole(owned, part_r)

    def folded(value):
        value = value + pltpu.roll(value, 4, 0)
        return value + pltpu.roll(value, 2, 0)

    rows = owned[0:8, :]
    for n in range(1, 8):
        rows += owned[8 * n : 8 * n + 8, :]
    mine[...] = folded(rows)

    @pl.loop(1, n_ex)
    def _(k):
        pltpu.make_async_remote_copy(
            mine.at[0:2, :], two(total, ex), own_s, own_r, device_id=(ex_at(k), me), device_id_type=MESH
        ).start()

    pltpu.make_async_copy(mine.at[0:2, :], two(total, ex), own_r).start()
    whole(total, own_r)
    out_ref[...] = folded(total[0:8, :] + total[8:16, :])[0:2, :]

    whole(yrecv.at[:, :, 0:896], act_s)
    whole(raw.at[0:124], val_s)
    whole(train.at[:, 0:62, :], train_s)
    whole(owned.at[0:62, :], part_s)
    whole(total.at[0:14, :], own_s)


def body(tokens, gates, routes, doc_ids, hidden_grad, proj_in, proj_out, val_features):
    n_dp, n_ex = lax.axis_size("dp"), lax.axis_size("expert")
    entries = proj_out.shape[0] * n_ex * proj_in.shape[1] ** 2
    dma = pltpu.SemaphoreType.DMA
    summed = pl.pallas_call(
        functools.partial(kernel, n_dp, n_ex),
        out_shape=jax.ShapeDtypeStruct((2, 128), F32),
        in_specs=[pl.BlockSpec(memory_space=pltpu.HBM)] * 8,
        out_specs=pl.BlockSpec(memory_space=pltpu.VMEM),
        scratch_shapes=[
            pltpu.VMEM((128, 4096), BF),
            pltpu.VMEM((8, 128), F32),
            pltpu.VMEM((8, 128), jnp.int32),
            pltpu.VMEM((1, 128), jnp.int32),
            pltpu.VMEM((2048, 1536), BF),
            pltpu.VMEM((64, 4096), BF),
            pltpu.VMEM((1024, 1536), BF),
            pltpu.VMEM((128, 128), F32),
            pltpu.VMEM((128, 128), F32),
            pltpu.VMEM((8, 2, 128, 128), BF),
            pltpu.VMEM((2, 128, 1024), BF),
            pltpu.VMEM((2, 1024, 512), BF),
            pltpu.VMEM((16, 64, 128), BF),
            pltpu.VMEM((128, 16, 128), BF),
            pltpu.VMEM((16, 128, 128), BF),
            pltpu.VMEM((16, 64, 128), BF),
            pltpu.VMEM((64, 128), F32),
            pltpu.VMEM((64, 128), F32),
            pltpu.VMEM((16, 128), F32),
            pltpu.VMEM((8, 128), F32),
            dma((5,)),
            dma((2, 8)),
        ]
        + [dma] * 10,
        compiler_params=pltpu.CompilerParams(
            collective_id=0, has_side_effects=True, vmem_limit_bytes=60 << 20
        ),
    )(
        tokens,
        gates.T,
        routes.T,
        doc_ids.reshape(1, -1),
        hidden_grad.reshape(-1, hidden_grad.shape[2]),
        proj_in.T,
        jnp.swapaxes(proj_out, 1, 2).reshape(-1, proj_out.shape[1]),
        val_features,
    )
    return summed * (1.0 / jnp.sqrt(F32(entries)))


def solution(mesh):
    in_specs = (
        P(("expert", "dp"), None),
        P(("expert", "dp"), None),
        P(("expert", "dp"), None),
        P(("expert", "dp")),
        P("expert", "dp", None),
        P(),
        P("expert", None, None),
        P("dp", "expert", None),
    )
    return jax.shard_map(body, mesh=mesh, in_specs=in_specs, out_specs=P("dp", None), check_vma=False)
```

```python
import functools

import jax
import jax.numpy as jnp
from jax import lax
from jax.experimental import pallas as pl
from jax.experimental.pallas import tpu as pltpu
from jax.sharding import PartitionSpec as P

MESH = pl.DeviceIdType.MESH
BF = jnp.bfloat16
F32 = jnp.float32
NT = (((1,), (1,)), ((), ()))
RING_Z = 8


def iota(shape, dim):
    return lax.broadcasted_iota(jnp.int32, shape, dim)


def dot(a, b):
    return jnp.dot(a, b, preferred_element_type=F32)


def dot_nt(a, b):
    return lax.dot_general(a, b, NT, preferred_element_type=F32)


def whole(ref, sem):
    pltpu.make_async_copy(ref, ref, sem).wait()


def kernel(
    n_dp, n_ex,
    tok_hbm, gate_hbm, route_hbm, doc_hbm, grad_hbm, pin_hbm, pout_hbm, val_hbm,
    out_ref,
    tok, gate, route, doc, grad, pin, pout,
    slots, gated, ysend, yrecv, diag, feats, raw, vals, train, part, owned, total, mine,
    in_sem, pair_sem, val_s, val_r, act_s, act_r, train_s, train_r, part_s, part_r, own_s, own_r,
):
    me = lax.axis_index("dp")
    ex = lax.axis_index("expert")

    def outward(k, n):
        return n // 2 + jnp.where(lax.rem(k, 2) == 0, k // 2, -((k + 1) // 2))

    def dp_at(k):
        x, z = me // RING_Z, lax.rem(me, RING_Z)
        x = lax.rem(x + outward(k // RING_Z, n_dp // RING_Z), n_dp // RING_Z)
        z = lax.rem(z + outward(lax.rem(k, RING_Z), RING_Z), RING_Z)
        return x * RING_Z + z

    def ex_at(k):
        return lax.rem(ex + k, n_ex)

    barrier = pltpu.get_barrier_semaphore()

    @pl.loop(0, n_dp - 1)
    def _(k):
        pl.semaphore_signal(barrier, inc=1, device_id=(ex, dp_at(k)), device_id_type=MESH)

    @pl.loop(1, n_ex)
    def _(k):
        pl.semaphore_signal(barrier, inc=1, device_id=(ex_at(k), me), device_id_type=MESH)

    loads = [
        pltpu.make_async_copy(src, dst, in_sem.at[n])
        for n, (src, dst) in enumerate(
            [(route_hbm, route), (gate_hbm, gate), (doc_hbm, doc), (pin_hbm, pin), (tok_hbm, tok)]
        )
    ]
    for load in loads:
        load.start()

    def pair_loads(c):
        rows, cols = pl.ds(pl.multiple_of(c * 256, 256), 256), pl.ds(pl.multiple_of(c * 128, 128), 128)
        return (
            pltpu.make_async_copy(grad_hbm.at[rows], grad.at[rows], pair_sem.at[0, c]),
            pltpu.make_async_copy(pout_hbm.at[cols], pout.at[cols], pair_sem.at[1, c]),
        )

    @pl.loop(0, 8)
    def _(c):
        for load in pair_loads(c):
            load.start()

    for load in loads[:3]:
        load.wait()
    experts = iota((128, 128), 0)
    named = jnp.zeros((128, 128), F32)
    weight = jnp.zeros((128, 128), F32)
    for k in range(8):
        hit = route[k : k + 1, :] == experts
        named = jnp.where(hit, 1.0, named)
        weight = jnp.where(hit, gate[k : k + 1, :], weight)
    earlier = (iota((128, 128), 0) < iota((128, 128), 1)).astype(BF)
    slots[...] = jnp.where(named > 0.0, dot(named.astype(BF), earlier), -1.0)
    gated[...] = weight

    @pl.loop(0, 16)
    def _(r):
        diag[:, pl.ds(pl.multiple_of(r * 64, 64), 64), :] = jnp.zeros((2, 64, 512), BF)

    for load in loads[3:]:
        load.wait()
    act = dot_nt(pin[...], tok[...])
    act_hi = act.astype(BF)
    act_lo = (act - act_hi.astype(F32)).astype(BF)
    row, col = iota((128, 64), 0), iota((128, 64), 1)
    spread = (col == 2 * ((row % 64) // 2) + row // 64).astype(BF)
    member = iota((128, 128), 0) % 2 == doc[...]
    x_hi = jnp.where(member, dot(spread, act_hi), 0.0).astype(BF)
    x_lo = jnp.where(member, dot(spread, act_lo), 0.0).astype(BF)

    place = iota((16, 128), 0).astype(F32)

    @pl.loop(0, n_ex)
    def _(g):
        blocks = []
        for e in range(16):
            at = pl.ds(g * 16 + e, 1)
            blocks.append(jnp.where(slots[at, :] == place, gated[at, :], 0.0))
        pick = jnp.concatenate(blocks, axis=0)
        pick_hi = pick.astype(BF)
        pick_lo = (pick - pick_hi.astype(F32)).astype(BF)
        y = dot_nt(x_hi, pick_hi) + dot_nt(x_lo, pick_hi) + dot_nt(x_hi, pick_lo)
        y = y.astype(BF)
        ysend[g, 0] = y[:, :128]
        ysend[g, 1] = y[:, 128:]

    pl.semaphore_wait(barrier, n_dp - 1 + n_ex - 1)

    def act_dst():
        return yrecv.at[:, :, pl.ds(pl.multiple_of(ex * 128, 128), 128)]

    @pl.loop(1, n_ex)
    def _(k):
        to = ex_at(k)
        pltpu.make_async_remote_copy(
            ysend.at[to], act_dst(), act_s, act_r, device_id=(to, me), device_id_type=MESH
        ).start()

    pltpu.make_async_copy(ysend.at[ex], act_dst(), act_r).start()

    def val_src(to):
        return val_hbm.at[:, :, pl.ds(pl.multiple_of(to * 128, 128), 128)]

    def val_dst():
        return raw.at[pl.ds(me * 4, 4)]

    @pl.loop(0, n_dp - 1)
    def _(k):
        to = dp_at(k)
        pltpu.make_async_remote_copy(
            val_src(to), val_dst(), val_s, val_r, device_id=(ex, to), device_id_type=MESH
        ).start()

    pltpu.make_async_copy(val_src(me), val_dst(), val_r).start()

    own_half = (iota((256, 128), 0) // 128) == (iota((256, 128), 1) // 64)

    @pl.loop(0, 8)
    def _(c):
        for load in pair_loads(c):
            load.wait()
        both = dot_nt(
            grad[pl.ds(pl.multiple_of(c * 256, 256), 256), :],
            pout[pl.ds(pl.multiple_of(c * 128, 128), 128), :],
        )
        both = jnp.where(own_half, both, 0.0).astype(BF)
        half, inner = c // 4, lax.rem(c, 4)
        cols = pl.ds(pl.multiple_of(inner * 128, 128), 128)
        for i in range(8):
            for e in range(2):
                rows = pl.ds(pl.multiple_of(i * 128 + inner * 32 + e * 16, 16), 16)
                diag[half, rows, cols] = both[e * 128 + i * 16 : e * 128 + i * 16 + 16, :]

    whole(yrecv, act_r)
    low = iota((64, 128), 1) < 64

    @pl.loop(0, 4)
    def _(q):
        half, inner = q // 2, lax.rem(q, 2)
        cols = pl.ds(pl.multiple_of(inner * 256, 256), 256)
        f = dot(yrecv[half], diag[half, :, cols])
        for h in range(2):
            even, odd = f[:64, h * 128 : h * 128 + 128], f[64:, h * 128 : h * 128 + 128]
            feats[4 * q + 2 * h] = jnp.where(low, even, pltpu.roll(odd, 64, 1)).astype(BF)
            feats[4 * q + 2 * h + 1] = jnp.where(low, pltpu.roll(even, 64, 1), odd).astype(BF)

    def pair(ref, at):
        return ref.at[:, pl.ds(at * 2, 2), :]

    @pl.loop(0, n_dp - 1)
    def _(k):
        to = dp_at(k)
        pltpu.make_async_remote_copy(
            pair(feats, to), pair(train, me), train_s, train_r, device_id=(ex, to), device_id_type=MESH
        ).start()

    pltpu.make_async_copy(pair(feats, me), pair(train, me), train_r).start()

    row, col = iota((256, 256), 0), iota((256, 256), 1)
    swap = ((row // 16 == col % 16) & (row % 16 == col // 16)).astype(BF)
    whole(raw, val_r)

    @pl.loop(0, 8)
    def _(b):
        at = pl.ds(pl.multiple_of(b * 16, 16), 16)
        turned = dot(swap, raw[at].reshape(256, 128)).astype(BF)
        for e in range(16):
            vals[e // 2, at, e % 2 * 128 : e % 2 * 128 + 128] = turned[e * 16 : e * 16 + 16, :]

    whole(train, train_r)
    score = jnp.zeros((64, 128), F32)
    for c in range(8):
        score += dot_nt(jnp.concatenate([train[2 * c], train[2 * c + 1]], axis=1), vals[c])
    part[...] = score

    def two(ref, at):
        return ref.at[pl.ds(at * 2, 2), :]

    @pl.loop(0, n_dp)
    def _(k):
        to = lax.rem(k, n_dp // RING_Z) * RING_Z + k // (n_dp // RING_Z)

        @pl.when(to != me)
        def _():
            pltpu.make_async_remote_copy(
                two(part, to), two(owned, me), part_s, part_r, device_id=(ex, to), device_id_type=MESH
            ).start()

        @pl.when(to == me)
        def _():
            pltpu.make_async_copy(two(part, me), two(owned, me), part_r).start()

    whole(owned, part_r)

    def folded(value):
        value = value + pltpu.roll(value, 4, 0)
        return value + pltpu.roll(value, 2, 0)

    rows = owned[0:8, :]
    for n in range(1, 8):
        rows += owned[8 * n : 8 * n + 8, :]
    mine[...] = folded(rows)

    @pl.loop(0, n_ex)
    def _(k):
        to = jnp.where(k < 2, 1 - k, k)

        @pl.when(to != ex)
        def _():
            pltpu.make_async_remote_copy(
                mine.at[0:2, :], two(total, ex), own_s, own_r, device_id=(to, me), device_id_type=MESH
            ).start()

    pltpu.make_async_copy(mine.at[0:2, :], two(total, ex), own_r).start()
    whole(total, own_r)
    out_ref[...] = folded(total[0:8, :] + total[8:16, :])[0:2, :]

    whole(yrecv.at[:, :, 0:896], act_s)
    whole(raw.at[0:124], val_s)
    whole(train.at[:, 0:62, :], train_s)
    whole(owned.at[0:62, :], part_s)
    whole(total.at[0:14, :], own_s)


def body(tokens, gates, routes, doc_ids, hidden_grad, proj_in, proj_out, val_features):
    n_dp, n_ex = lax.axis_size("dp"), lax.axis_size("expert")
    entries = proj_out.shape[0] * n_ex * proj_in.shape[1] ** 2
    dma = pltpu.SemaphoreType.DMA
    summed = pl.pallas_call(
        functools.partial(kernel, n_dp, n_ex),
        out_shape=jax.ShapeDtypeStruct((2, 128), F32),
        in_specs=[pl.BlockSpec(memory_space=pltpu.HBM)] * 8,
        out_specs=pl.BlockSpec(memory_space=pltpu.VMEM),
        scratch_shapes=[
            pltpu.VMEM((128, 4096), BF),
            pltpu.VMEM((8, 128), F32),
            pltpu.VMEM((8, 128), jnp.int32),
            pltpu.VMEM((1, 128), jnp.int32),
            pltpu.VMEM((2048, 1536), BF),
            pltpu.VMEM((64, 4096), BF),
            pltpu.VMEM((1024, 1536), BF),
            pltpu.VMEM((128, 128), F32),
            pltpu.VMEM((128, 128), F32),
            pltpu.VMEM((8, 2, 128, 128), BF),
            pltpu.VMEM((2, 128, 1024), BF),
            pltpu.VMEM((2, 1024, 512), BF),
            pltpu.VMEM((16, 64, 128), BF),
            pltpu.VMEM((128, 16, 128), BF),
            pltpu.VMEM((8, 128, 256), BF),
            pltpu.VMEM((16, 64, 128), BF),
            pltpu.VMEM((64, 128), F32),
            pltpu.VMEM((64, 128), F32),
            pltpu.VMEM((16, 128), F32),
            pltpu.VMEM((8, 128), F32),
            dma((5,)),
            dma((2, 8)),
        ]
        + [dma] * 10,
        compiler_params=pltpu.CompilerParams(
            collective_id=0, has_side_effects=True, vmem_limit_bytes=60 << 20
        ),
    )(
        tokens,
        gates.T,
        routes.T,
        doc_ids.reshape(1, -1),
        hidden_grad.reshape(-1, hidden_grad.shape[2]),
        proj_in.T,
        jnp.swapaxes(proj_out, 1, 2).reshape(-1, proj_out.shape[1]),
        val_features,
    )
    return summed * (1.0 / jnp.sqrt(F32(entries)))


def solution(mesh):
    in_specs = (
        P(("expert", "dp"), None),
        P(("expert", "dp"), None),
        P(("expert", "dp"), None),
        P(("expert", "dp")),
        P("expert", "dp", None),
        P(),
        P("expert", None, None),
        P("dp", "expert", None),
    )
    return jax.shard_map(body, mesh=mesh, in_specs=in_specs, out_specs=P("dp", None), check_vma=False)
```

```python
import functools

import jax
import jax.numpy as jnp
from jax import lax
from jax.experimental import pallas as pl
from jax.experimental.pallas import tpu as pltpu
from jax.sharding import PartitionSpec as P

MESH = pl.DeviceIdType.MESH
BF = jnp.bfloat16
F32 = jnp.float32
NT = (((1,), (1,)), ((), ()))
RING_Z = 8


def iota(shape, dim):
    return lax.broadcasted_iota(jnp.int32, shape, dim)


def dot(a, b):
    return jnp.dot(a, b, preferred_element_type=F32)


def dot_nt(a, b):
    return lax.dot_general(a, b, NT, preferred_element_type=F32)


def whole(ref, sem):
    pltpu.make_async_copy(ref, ref, sem).wait()


def kernel(
    n_dp, n_ex,
    tok_hbm, gate_hbm, route_hbm, doc_hbm, grad_hbm, pin_hbm, pout_hbm, val_hbm,
    out_ref,
    tok, gate, route, doc, grad, pin, pout,
    slots, gated, ysend, yrecv, diag, feats, raw, vals, train, part, owned, total, mine,
    in_sem, pair_sem, val_s, val_r, act_s, act_r, train_s, train_r, part_s, part_r, own_s, own_r,
):
    me = lax.axis_index("dp")
    ex = lax.axis_index("expert")

    def outward(k, n):
        return n // 2 + jnp.where(lax.rem(k, 2) == 0, k // 2, -((k + 1) // 2))

    def dp_at(k):
        x, z = me // RING_Z, lax.rem(me, RING_Z)
        x = lax.rem(x + outward(k // RING_Z, n_dp // RING_Z), n_dp // RING_Z)
        z = lax.rem(z + outward(lax.rem(k, RING_Z), RING_Z), RING_Z)
        return x * RING_Z + z

    def ex_at(k):
        return lax.rem(ex + k, n_ex)

    barrier = pltpu.get_barrier_semaphore()

    @pl.loop(0, n_dp - 1)
    def _(k):
        pl.semaphore_signal(barrier, inc=1, device_id=(ex, dp_at(k)), device_id_type=MESH)

    @pl.loop(1, n_ex)
    def _(k):
        pl.semaphore_signal(barrier, inc=1, device_id=(ex_at(k), me), device_id_type=MESH)

    loads = [
        pltpu.make_async_copy(src, dst, in_sem.at[n])
        for n, (src, dst) in enumerate(
            [(route_hbm, route), (gate_hbm, gate), (doc_hbm, doc), (pin_hbm, pin), (tok_hbm, tok)]
        )
    ]
    for load in loads:
        load.start()

    def pair_loads(c):
        rows, cols = pl.ds(pl.multiple_of(c * 256, 256), 256), pl.ds(pl.multiple_of(c * 128, 128), 128)
        return (
            pltpu.make_async_copy(grad_hbm.at[rows], grad.at[rows], pair_sem.at[0, c]),
            pltpu.make_async_copy(pout_hbm.at[cols], pout.at[cols], pair_sem.at[1, c]),
        )

    @pl.loop(0, 8)
    def _(c):
        for load in pair_loads(c):
            load.start()

    for load in loads[:3]:
        load.wait()
    experts = iota((128, 128), 0)
    named = jnp.zeros((128, 128), F32)
    weight = jnp.zeros((128, 128), F32)
    for k in range(8):
        hit = route[k : k + 1, :] == experts
        named = jnp.where(hit, 1.0, named)
        weight = jnp.where(hit, gate[k : k + 1, :], weight)
    earlier = (iota((128, 128), 0) < iota((128, 128), 1)).astype(BF)
    slots[...] = jnp.where(named > 0.0, dot(named.astype(BF), earlier), -1.0)
    gated[...] = weight

    for load in loads[3:]:
        load.wait()
    act = dot_nt(pin[...], tok[...])
    act_hi = act.astype(BF)
    act_lo = (act - act_hi.astype(F32)).astype(BF)
    row, col = iota((128, 64), 0), iota((128, 64), 1)
    spread = (col == 2 * ((row % 64) // 2) + row // 64).astype(BF)
    member = iota((128, 128), 0) % 2 == doc[...]
    x_hi = jnp.where(member, dot(spread, act_hi), 0.0).astype(BF)
    x_lo = jnp.where(member, dot(spread, act_lo), 0.0).astype(BF)

    x_both = jnp.concatenate([x_hi, x_lo], axis=1)

    pl.semaphore_wait(barrier, n_dp - 1 + n_ex - 1)

    def val_src(to):
        return val_hbm.at[:, :, pl.ds(pl.multiple_of(to * 128, 128), 128)]

    def val_dst():
        return raw.at[pl.ds(me * 4, 4)]

    @pl.loop(0, 20)
    def _(k):
        to = dp_at(k)
        pltpu.make_async_remote_copy(
            val_src(to), val_dst(), val_s, val_r, device_id=(ex, to), device_id_type=MESH
        ).start()

    place = iota((16, 128), 0).astype(F32)

    @pl.loop(0, n_ex)
    def _(g):
        blocks = []
        for e in range(16):
            at = pl.ds(g * 16 + e, 1)
            blocks.append(jnp.where(slots[at, :] == place, gated[at, :], 0.0))
        pick = jnp.concatenate(blocks, axis=0)
        pick_hi = pick.astype(BF)
        pick_lo = (pick - pick_hi.astype(F32)).astype(BF)
        y = dot_nt(x_both, jnp.concatenate([pick_hi, pick_hi], axis=1)) + dot_nt(x_hi, pick_lo)
        y = y.astype(BF)
        ysend[g, 0] = y[:, :128]
        ysend[g, 1] = y[:, 128:]

    def act_dst():
        return yrecv.at[:, :, pl.ds(pl.multiple_of(ex * 128, 128), 128)]

    @pl.loop(1, n_ex)
    def _(k):
        to = ex_at(k)
        pltpu.make_async_remote_copy(
            ysend.at[to], act_dst(), act_s, act_r, device_id=(to, me), device_id_type=MESH
        ).start()

    pltpu.make_async_copy(ysend.at[ex], act_dst(), act_r).start()

    @pl.loop(20, n_dp - 1)
    def _(k):
        to = dp_at(k)
        pltpu.make_async_remote_copy(
            val_src(to), val_dst(), val_s, val_r, device_id=(ex, to), device_id_type=MESH
        ).start()

    pltpu.make_async_copy(val_src(me), val_dst(), val_r).start()

    @pl.loop(0, 16)
    def _(r):
        diag[:, pl.ds(pl.multiple_of(r * 64, 64), 64), :] = jnp.zeros((2, 64, 512), BF)

    own_half = (iota((256, 128), 0) // 128) == (iota((256, 128), 1) // 64)

    @pl.loop(0, 8)
    def _(c):
        for load in pair_loads(c):
            load.wait()
        both = dot_nt(
            grad[pl.ds(pl.multiple_of(c * 256, 256), 256), :],
            pout[pl.ds(pl.multiple_of(c * 128, 128), 128), :],
        )
        both = jnp.where(own_half, both, 0.0).astype(BF)
        half, inner = c // 4, lax.rem(c, 4)
        cols = pl.ds(pl.multiple_of(inner * 128, 128), 128)
        for i in range(8):
            for e in range(2):
                rows = pl.ds(pl.multiple_of(i * 128 + inner * 32 + e * 16, 16), 16)
                diag[half, rows, cols] = both[e * 128 + i * 16 : e * 128 + i * 16 + 16, :]

    whole(yrecv, act_r)
    low = iota((64, 128), 1) < 64

    @pl.loop(0, 4)
    def _(q):
        half, inner = q // 2, lax.rem(q, 2)
        cols = pl.ds(pl.multiple_of(inner * 256, 256), 256)
        f = dot(yrecv[half], diag[half, :, cols])
        for h in range(2):
            even, odd = f[:64, h * 128 : h * 128 + 128], f[64:, h * 128 : h * 128 + 128]
            feats[4 * q + 2 * h] = jnp.where(low, even, pltpu.roll(odd, 64, 1)).astype(BF)
            feats[4 * q + 2 * h + 1] = jnp.where(low, pltpu.roll(even, 64, 1), odd).astype(BF)

    def pair(ref, at):
        return ref.at[:, pl.ds(at * 2, 2), :]

    @pl.loop(0, n_dp - 1)
    def _(k):
        to = dp_at(k)
        pltpu.make_async_remote_copy(
            pair(feats, to), pair(train, me), train_s, train_r, device_id=(ex, to), device_id_type=MESH
        ).start()

    pltpu.make_async_copy(pair(feats, me), pair(train, me), train_r).start()

    row, col = iota((256, 256), 0), iota((256, 256), 1)
    swap = ((row // 16 == col % 16) & (row % 16 == col // 16)).astype(BF)
    whole(raw, val_r)

    @pl.loop(0, 8)
    def _(b):
        at = pl.ds(pl.multiple_of(b * 16, 16), 16)
        turned = dot(swap, raw[at].reshape(256, 128)).astype(BF)
        for e in range(16):
            vals[e // 2, at, e % 2 * 128 : e % 2 * 128 + 128] = turned[e * 16 : e * 16 + 16, :]

    whole(train, train_r)
    score = jnp.zeros((64, 128), F32)
    for c in range(8):
        score += dot_nt(jnp.concatenate([train[2 * c], train[2 * c + 1]], axis=1), vals[c])
    part[...] = score

    def two(ref, at):
        return ref.at[pl.ds(at * 2, 2), :]

    @pl.loop(0, n_dp)
    def _(k):
        to = lax.rem(k, n_dp // RING_Z) * RING_Z + k // (n_dp // RING_Z)

        @pl.when(to != me)
        def _():
            pltpu.make_async_remote_copy(
                two(part, to), two(owned, me), part_s, part_r, device_id=(ex, to), device_id_type=MESH
            ).start()

        @pl.when(to == me)
        def _():
            pltpu.make_async_copy(two(part, me), two(owned, me), part_r).start()

    whole(owned, part_r)

    def folded(value):
        value = value + pltpu.roll(value, 4, 0)
        return value + pltpu.roll(value, 2, 0)

    rows = owned[0:8, :]
    for n in range(1, 8):
        rows += owned[8 * n : 8 * n + 8, :]
    mine[...] = folded(rows)

    @pl.loop(0, n_ex)
    def _(k):
        to = jnp.where(k < 2, 1 - k, k)

        @pl.when(to != ex)
        def _():
            pltpu.make_async_remote_copy(
                mine.at[0:2, :], two(total, ex), own_s, own_r, device_id=(to, me), device_id_type=MESH
            ).start()

    pltpu.make_async_copy(mine.at[0:2, :], two(total, ex), own_r).start()
    whole(total, own_r)
    out_ref[...] = folded(total[0:8, :] + total[8:16, :])[0:2, :]

    whole(yrecv.at[:, :, 0:896], act_s)
    whole(raw.at[0:124], val_s)
    whole(train.at[:, 0:62, :], train_s)
    whole(owned.at[0:62, :], part_s)
    whole(total.at[0:14, :], own_s)


def body(tokens, gates, routes, doc_ids, hidden_grad, proj_in, proj_out, val_features):
    n_dp, n_ex = lax.axis_size("dp"), lax.axis_size("expert")
    entries = proj_out.shape[0] * n_ex * proj_in.shape[1] ** 2
    dma = pltpu.SemaphoreType.DMA
    summed = pl.pallas_call(
        functools.partial(kernel, n_dp, n_ex),
        out_shape=jax.ShapeDtypeStruct((2, 128), F32),
        in_specs=[pl.BlockSpec(memory_space=pltpu.HBM)] * 8,
        out_specs=pl.BlockSpec(memory_space=pltpu.VMEM),
        scratch_shapes=[
            pltpu.VMEM((128, 4096), BF),
            pltpu.VMEM((8, 128), F32),
            pltpu.VMEM((8, 128), jnp.int32),
            pltpu.VMEM((1, 128), jnp.int32),
            pltpu.VMEM((2048, 1536), BF),
            pltpu.VMEM((64, 4096), BF),
            pltpu.VMEM((1024, 1536), BF),
            pltpu.VMEM((128, 128), F32),
            pltpu.VMEM((128, 128), F32),
            pltpu.VMEM((8, 2, 128, 128), BF),
            pltpu.VMEM((2, 128, 1024), BF),
            pltpu.VMEM((2, 1024, 512), BF),
            pltpu.VMEM((16, 64, 128), BF),
            pltpu.VMEM((128, 16, 128), BF),
            pltpu.VMEM((8, 128, 256), BF),
            pltpu.VMEM((16, 64, 128), BF),
            pltpu.VMEM((64, 128), F32),
            pltpu.VMEM((64, 128), F32),
            pltpu.VMEM((16, 128), F32),
            pltpu.VMEM((8, 128), F32),
            dma((5,)),
            dma((2, 8)),
        ]
        + [dma] * 10,
        compiler_params=pltpu.CompilerParams(
            collective_id=0, has_side_effects=True, vmem_limit_bytes=60 << 20
        ),
    )(
        tokens,
        gates.T,
        routes.T,
        doc_ids.reshape(1, -1),
        hidden_grad.reshape(-1, hidden_grad.shape[2]),
        proj_in.T,
        jnp.swapaxes(proj_out, 1, 2).reshape(-1, proj_out.shape[1]),
        val_features,
    )
    return summed * (1.0 / jnp.sqrt(F32(entries)))


def solution(mesh):
    in_specs = (
        P(("expert", "dp"), None),
        P(("expert", "dp"), None),
        P(("expert", "dp"), None),
        P(("expert", "dp")),
        P("expert", "dp", None),
        P(),
        P("expert", None, None),
        P("dp", "expert", None),
    )
    return jax.shard_map(body, mesh=mesh, in_specs=in_specs, out_specs=P("dp", None), check_vma=False)
```

```python
import functools

import jax
import jax.numpy as jnp
from jax import lax
from jax.experimental import pallas as pl
from jax.experimental.pallas import tpu as pltpu
from jax.sharding import PartitionSpec as P

MESH = pl.DeviceIdType.MESH
BF = jnp.bfloat16
F32 = jnp.float32
NT = (((1,), (1,)), ((), ()))
RING_Z = 8


def iota(shape, dim):
    return lax.broadcasted_iota(jnp.int32, shape, dim)


def dot(a, b):
    return jnp.dot(a, b, preferred_element_type=F32)


def dot_nt(a, b):
    return lax.dot_general(a, b, NT, preferred_element_type=F32)


def whole(ref, sem):
    pltpu.make_async_copy(ref, ref, sem).wait()


def kernel(
    n_dp, n_ex,
    tok_hbm, gate_hbm, route_hbm, doc_hbm, grad_hbm, pin_hbm, pout_hbm, val_hbm,
    out_ref,
    tok, gate, route, doc, grad, pin, pout,
    slots, gated, ysend, yrecv, diag, feats, raw, vals, train, part, owned, total, mine,
    in_sem, pair_sem, val_s, val_r, act_s, act_r, train_s, train_r, part_s, part_r, own_s, own_r,
):
    me = lax.axis_index("dp")
    ex = lax.axis_index("expert")

    def outward(k, n):
        return n // 2 + jnp.where(lax.rem(k, 2) == 0, k // 2, -((k + 1) // 2))

    def dp_at(k):
        x, z = me // RING_Z, lax.rem(me, RING_Z)
        x = lax.rem(x + outward(k // RING_Z, n_dp // RING_Z), n_dp // RING_Z)
        z = lax.rem(z + outward(lax.rem(k, RING_Z), RING_Z), RING_Z)
        return x * RING_Z + z

    def ex_at(k):
        return lax.rem(ex + k, n_ex)

    barrier = pltpu.get_barrier_semaphore()

    @pl.loop(0, n_dp - 1)
    def _(k):
        pl.semaphore_signal(barrier, inc=1, device_id=(ex, dp_at(k)), device_id_type=MESH)

    @pl.loop(1, n_ex)
    def _(k):
        pl.semaphore_signal(barrier, inc=1, device_id=(ex_at(k), me), device_id_type=MESH)

    loads = [
        pltpu.make_async_copy(src, dst, in_sem.at[n])
        for n, (src, dst) in enumerate(
            [(route_hbm, route), (gate_hbm, gate), (doc_hbm, doc), (pin_hbm, pin), (tok_hbm, tok)]
        )
    ]
    for load in loads:
        load.start()

    def pair_loads(c):
        rows, cols = pl.ds(pl.multiple_of(c * 256, 256), 256), pl.ds(pl.multiple_of(c * 128, 128), 128)
        return (
            pltpu.make_async_copy(grad_hbm.at[rows], grad.at[rows], pair_sem.at[0, c]),
            pltpu.make_async_copy(pout_hbm.at[cols], pout.at[cols], pair_sem.at[1, c]),
        )

    @pl.loop(0, 8)
    def _(c):
        for load in pair_loads(c):
            load.start()

    pl.semaphore_wait(barrier, n_dp - 1 + n_ex - 1)

    def val_src(to):
        return val_hbm.at[:, :, pl.ds(pl.multiple_of(to * 128, 128), 128)]

    def val_dst():
        return raw.at[pl.ds(me * 4, 4)]

    @pl.loop(0, 20)
    def _(k):
        to = dp_at(k)
        pltpu.make_async_remote_copy(
            val_src(to), val_dst(), val_s, val_r, device_id=(ex, to), device_id_type=MESH
        ).start()

    for load in loads[:3]:
        load.wait()
    experts = iota((128, 128), 0)
    named = jnp.zeros((128, 128), F32)
    weight = jnp.zeros((128, 128), F32)
    for k in range(8):
        hit = route[k : k + 1, :] == experts
        named = jnp.where(hit, 1.0, named)
        weight = jnp.where(hit, gate[k : k + 1, :], weight)
    earlier = (iota((128, 128), 0) < iota((128, 128), 1)).astype(BF)
    slots[...] = jnp.where(named > 0.0, dot(named.astype(BF), earlier), -1.0)
    gated[...] = weight

    for load in loads[3:]:
        load.wait()
    act = dot_nt(pin[...], tok[...])
    act_hi = act.astype(BF)
    act_lo = (act - act_hi.astype(F32)).astype(BF)
    row, col = iota((128, 64), 0), iota((128, 64), 1)
    spread = (col == 2 * ((row % 64) // 2) + row // 64).astype(BF)
    member = iota((128, 128), 0) % 2 == doc[...]
    x_hi = jnp.where(member, dot(spread, act_hi), 0.0).astype(BF)
    x_lo = jnp.where(member, dot(spread, act_lo), 0.0).astype(BF)

    x_both = jnp.concatenate([x_hi, x_lo], axis=1)

    place = iota((16, 128), 0).astype(F32)

    @pl.loop(0, n_ex)
    def _(g):
        blocks = []
        for e in range(16):
            at = pl.ds(g * 16 + e, 1)
            blocks.append(jnp.where(slots[at, :] == place, gated[at, :], 0.0))
        pick = jnp.concatenate(blocks, axis=0)
        pick_hi = pick.astype(BF)
        pick_lo = (pick - pick_hi.astype(F32)).astype(BF)
        y = dot_nt(x_both, jnp.concatenate([pick_hi, pick_hi], axis=1)) + dot_nt(x_hi, pick_lo)
        y = y.astype(BF)
        ysend[g, 0] = y[:, :128]
        ysend[g, 1] = y[:, 128:]

    def act_dst():
        return yrecv.at[:, :, pl.ds(pl.multiple_of(ex * 128, 128), 128)]

    @pl.loop(1, n_ex)
    def _(k):
        to = ex_at(k)
        pltpu.make_async_remote_copy(
            ysend.at[to], act_dst(), act_s, act_r, device_id=(to, me), device_id_type=MESH
        ).start()

    pltpu.make_async_copy(ysend.at[ex], act_dst(), act_r).start()

    @pl.loop(20, n_dp - 1)
    def _(k):
        to = dp_at(k)
        pltpu.make_async_remote_copy(
            val_src(to), val_dst(), val_s, val_r, device_id=(ex, to), device_id_type=MESH
        ).start()

    pltpu.make_async_copy(val_src(me), val_dst(), val_r).start()

    @pl.loop(0, 16)
    def _(r):
        diag[:, pl.ds(pl.multiple_of(r * 64, 64), 64), :] = jnp.zeros((2, 64, 512), BF)

    own_half = (iota((256, 128), 0) // 128) == (iota((256, 128), 1) // 64)

    @pl.loop(0, 8)
    def _(c):
        for load in pair_loads(c):
            load.wait()
        both = dot_nt(
            grad[pl.ds(pl.multiple_of(c * 256, 256), 256), :],
            pout[pl.ds(pl.multiple_of(c * 128, 128), 128), :],
        )
        both = jnp.where(own_half, both, 0.0).astype(BF)
        half, inner = c // 4, lax.rem(c, 4)
        cols = pl.ds(pl.multiple_of(inner * 128, 128), 128)
        for i in range(8):
            for e in range(2):
                rows = pl.ds(pl.multiple_of(i * 128 + inner * 32 + e * 16, 16), 16)
                diag[half, rows, cols] = both[e * 128 + i * 16 : e * 128 + i * 16 + 16, :]

    whole(yrecv, act_r)
    low = iota((64, 128), 1) < 64

    @pl.loop(0, 4)
    def _(q):
        half, inner = q // 2, lax.rem(q, 2)
        cols = pl.ds(pl.multiple_of(inner * 256, 256), 256)
        f = dot(yrecv[half], diag[half, :, cols])
        for h in range(2):
            even, odd = f[:64, h * 128 : h * 128 + 128], f[64:, h * 128 : h * 128 + 128]
            feats[4 * q + 2 * h] = jnp.where(low, even, pltpu.roll(odd, 64, 1)).astype(BF)
            feats[4 * q + 2 * h + 1] = jnp.where(low, pltpu.roll(even, 64, 1), odd).astype(BF)

    def pair(ref, at):
        return ref.at[:, pl.ds(at * 2, 2), :]

    @pl.loop(0, n_dp - 1)
    def _(k):
        to = dp_at(k)
        pltpu.make_async_remote_copy(
            pair(feats, to), pair(train, me), train_s, train_r, device_id=(ex, to), device_id_type=MESH
        ).start()

    pltpu.make_async_copy(pair(feats, me), pair(train, me), train_r).start()

    row, col = iota((256, 256), 0), iota((256, 256), 1)
    swap = ((row // 16 == col % 16) & (row % 16 == col // 16)).astype(BF)
    whole(raw, val_r)

    @pl.loop(0, 8)
    def _(b):
        at = pl.ds(pl.multiple_of(b * 16, 16), 16)
        turned = dot(swap, raw[at].reshape(256, 128)).astype(BF)
        for e in range(16):
            vals[e // 2, at, e % 2 * 128 : e % 2 * 128 + 128] = turned[e * 16 : e * 16 + 16, :]

    whole(train, train_r)
    score = jnp.zeros((64, 128), F32)
    for c in range(8):
        score += dot_nt(jnp.concatenate([train[2 * c], train[2 * c + 1]], axis=1), vals[c])
    part[...] = score

    def two(ref, at):
        return ref.at[pl.ds(at * 2, 2), :]

    @pl.loop(0, n_dp - 1)
    def _(k):
        turn = me % RING_Z * (n_dp // RING_Z) + me // RING_Z
        k = jnp.where(k >= turn, k + 1, k)
        to = lax.rem(k, n_dp // RING_Z) * RING_Z + k // (n_dp // RING_Z)
        pltpu.make_async_remote_copy(
            two(part, to), two(owned, me), part_s, part_r, device_id=(ex, to), device_id_type=MESH
        ).start()

    pltpu.make_async_copy(two(part, me), two(owned, me), part_r).start()
    whole(owned, part_r)

    def folded(value):
        value = value + pltpu.roll(value, 4, 0)
        return value + pltpu.roll(value, 2, 0)

    rows = owned[0:8, :]
    for n in range(1, 8):
        rows += owned[8 * n : 8 * n + 8, :]
    mine[...] = folded(rows)

    @pl.loop(0, n_ex)
    def _(k):
        to = jnp.where(k < 2, 1 - k, k)

        @pl.when(to != ex)
        def _():
            pltpu.make_async_remote_copy(
                mine.at[0:2, :], two(total, ex), own_s, own_r, device_id=(to, me), device_id_type=MESH
            ).start()

    pltpu.make_async_copy(mine.at[0:2, :], two(total, ex), own_r).start()
    whole(total, own_r)
    out_ref[...] = folded(total[0:8, :] + total[8:16, :])[0:2, :]

    whole(yrecv.at[:, :, 0:896], act_s)
    whole(raw.at[0:124], val_s)
    whole(train.at[:, 0:62, :], train_s)
    whole(owned.at[0:62, :], part_s)
    whole(total.at[0:14, :], own_s)


def body(tokens, gates, routes, doc_ids, hidden_grad, proj_in, proj_out, val_features):
    n_dp, n_ex = lax.axis_size("dp"), lax.axis_size("expert")
    entries = proj_out.shape[0] * n_ex * proj_in.shape[1] ** 2
    dma = pltpu.SemaphoreType.DMA
    summed = pl.pallas_call(
        functools.partial(kernel, n_dp, n_ex),
        out_shape=jax.ShapeDtypeStruct((2, 128), F32),
        in_specs=[pl.BlockSpec(memory_space=pltpu.HBM)] * 8,
        out_specs=pl.BlockSpec(memory_space=pltpu.VMEM),
        scratch_shapes=[
            pltpu.VMEM((128, 4096), BF),
            pltpu.VMEM((8, 128), F32),
            pltpu.VMEM((8, 128), jnp.int32),
            pltpu.VMEM((1, 128), jnp.int32),
            pltpu.VMEM((2048, 1536), BF),
            pltpu.VMEM((64, 4096), BF),
            pltpu.VMEM((1024, 1536), BF),
            pltpu.VMEM((128, 128), F32),
            pltpu.VMEM((128, 128), F32),
            pltpu.VMEM((8, 2, 128, 128), BF),
            pltpu.VMEM((2, 128, 1024), BF),
            pltpu.VMEM((2, 1024, 512), BF),
            pltpu.VMEM((16, 64, 128), BF),
            pltpu.VMEM((128, 16, 128), BF),
            pltpu.VMEM((8, 128, 256), BF),
            pltpu.VMEM((16, 64, 128), BF),
            pltpu.VMEM((64, 128), F32),
            pltpu.VMEM((64, 128), F32),
            pltpu.VMEM((16, 128), F32),
            pltpu.VMEM((8, 128), F32),
            dma((5,)),
            dma((2, 8)),
        ]
        + [dma] * 10,
        compiler_params=pltpu.CompilerParams(
            collective_id=0, has_side_effects=True, vmem_limit_bytes=60 << 20
        ),
    )(
        tokens,
        gates.T,
        routes.T,
        doc_ids.reshape(1, -1),
        hidden_grad.reshape(-1, hidden_grad.shape[2]),
        proj_in.T,
        jnp.swapaxes(proj_out, 1, 2).reshape(-1, proj_out.shape[1]),
        val_features,
    )
    return summed * (1.0 / jnp.sqrt(F32(entries)))


def solution(mesh):
    in_specs = (
        P(("expert", "dp"), None),
        P(("expert", "dp"), None),
        P(("expert", "dp"), None),
        P(("expert", "dp")),
        P("expert", "dp", None),
        P(),
        P("expert", None, None),
        P("dp", "expert", None),
    )
    return jax.shard_map(body, mesh=mesh, in_specs=in_specs, out_specs=P("dp", None), check_vma=False)
```

```python
import functools

import jax
import jax.numpy as jnp
from jax import lax
from jax.experimental import pallas as pl
from jax.experimental.pallas import tpu as pltpu
from jax.sharding import PartitionSpec as P

MESH = pl.DeviceIdType.MESH
BF = jnp.bfloat16
F32 = jnp.float32
NT = (((1,), (1,)), ((), ()))
RING_Z = 8


def iota(shape, dim):
    return lax.broadcasted_iota(jnp.int32, shape, dim)


def dot(a, b):
    return jnp.dot(a, b, preferred_element_type=F32)


def dot_nt(a, b):
    return lax.dot_general(a, b, NT, preferred_element_type=F32)


def whole(ref, sem):
    pltpu.make_async_copy(ref, ref, sem).wait()


def kernel(
    n_dp, n_ex,
    tok_hbm, gate_hbm, route_hbm, doc_hbm, grad_hbm, pin_hbm, pout_hbm, val_hbm,
    out_ref,
    tok, gate, route, doc, grad, pin, pout,
    slots, gated, ysend, yrecv, diag, feats, raw, vals, train, part, owned, total, mine,
    in_sem, pair_sem, val_s, val_r, act_s, act_r, train_s, train_r, part_s, part_r, own_s, own_r,
):
    me = lax.axis_index("dp")
    ex = lax.axis_index("expert")

    def outward(k, n):
        return n // 2 + jnp.where(lax.rem(k, 2) == 0, k // 2, -((k + 1) // 2))

    def dp_at(k):
        x, z = me // RING_Z, lax.rem(me, RING_Z)
        x = lax.rem(x + outward(k // RING_Z, n_dp // RING_Z), n_dp // RING_Z)
        z = lax.rem(z + outward(lax.rem(k, RING_Z), RING_Z), RING_Z)
        return x * RING_Z + z

    def ex_at(k):
        return lax.rem(ex + k, n_ex)

    barrier = pltpu.get_barrier_semaphore()

    @pl.loop(0, n_dp - 1)
    def _(k):
        pl.semaphore_signal(barrier, inc=1, device_id=(ex, dp_at(k)), device_id_type=MESH)

    @pl.loop(1, n_ex)
    def _(k):
        pl.semaphore_signal(barrier, inc=1, device_id=(ex_at(k), me), device_id_type=MESH)

    loads = [
        pltpu.make_async_copy(src, dst, in_sem.at[n])
        for n, (src, dst) in enumerate(
            [(route_hbm, route), (gate_hbm, gate), (doc_hbm, doc), (pin_hbm, pin), (tok_hbm, tok)]
        )
    ]
    for load in loads:
        load.start()

    def pair_loads(c):
        rows, cols = pl.ds(pl.multiple_of(c * 256, 256), 256), pl.ds(pl.multiple_of(c * 128, 128), 128)
        return (
            pltpu.make_async_copy(grad_hbm.at[rows], grad.at[rows], pair_sem.at[0, c]),
            pltpu.make_async_copy(pout_hbm.at[cols], pout.at[cols], pair_sem.at[1, c]),
        )

    @pl.loop(0, 8)
    def _(c):
        for load in pair_loads(c):
            load.start()

    pl.semaphore_wait(barrier, n_dp - 1 + n_ex - 1)

    def val_src(to):
        return val_hbm.at[:, :, pl.ds(pl.multiple_of(to * 128, 128), 128)]

    def val_dst():
        return raw.at[pl.ds(me * 4, 4)]

    @pl.loop(0, 12)
    def _(k):
        to = dp_at(k)
        pltpu.make_async_remote_copy(
            val_src(to), val_dst(), val_s, val_r, device_id=(ex, to), device_id_type=MESH
        ).start()

    for load in loads[:3]:
        load.wait()
    experts = iota((128, 128), 0)
    named = jnp.zeros((128, 128), F32)
    weight = jnp.zeros((128, 128), F32)
    for k in range(8):
        hit = route[k : k + 1, :] == experts
        named = jnp.where(hit, 1.0, named)
        weight = jnp.where(hit, gate[k : k + 1, :], weight)
    earlier = (iota((128, 128), 0) < iota((128, 128), 1)).astype(BF)
    slots[...] = jnp.where(named > 0.0, dot(named.astype(BF), earlier), -1.0)
    gated[...] = weight

    for load in loads[3:]:
        load.wait()
    act = dot_nt(pin[...], tok[...])
    act_hi = act.astype(BF)
    act_lo = (act - act_hi.astype(F32)).astype(BF)
    row, col = iota((128, 64), 0), iota((128, 64), 1)
    spread = (col == 2 * ((row % 64) // 2) + row // 64).astype(BF)
    member = iota((128, 128), 0) % 2 == doc[...]
    x_hi = jnp.where(member, dot(spread, act_hi), 0.0).astype(BF)
    x_lo = jnp.where(member, dot(spread, act_lo), 0.0).astype(BF)

    x_both = jnp.concatenate([x_hi, x_lo], axis=1)

    place = iota((16, 128), 0).astype(F32)

    @pl.loop(0, n_ex)
    def _(g):
        blocks = []
        for e in range(16):
            at = pl.ds(g * 16 + e, 1)
            blocks.append(jnp.where(slots[at, :] == place, gated[at, :], 0.0))
        pick = jnp.concatenate(blocks, axis=0)
        pick_hi = pick.astype(BF)
        pick_lo = (pick - pick_hi.astype(F32)).astype(BF)
        y = dot_nt(x_both, jnp.concatenate([pick_hi, pick_hi], axis=1)) + dot_nt(x_hi, pick_lo)
        y = y.astype(BF)
        ysend[g, 0] = y[:, :128]
        ysend[g, 1] = y[:, 128:]

    def act_dst():
        return yrecv.at[:, :, pl.ds(pl.multiple_of(ex * 128, 128), 128)]

    @pl.loop(1, n_ex)
    def _(k):
        to = ex_at(k)
        pltpu.make_async_remote_copy(
            ysend.at[to], act_dst(), act_s, act_r, device_id=(to, me), device_id_type=MESH
        ).start()

    pltpu.make_async_copy(ysend.at[ex], act_dst(), act_r).start()

    @pl.loop(12, n_dp - 1)
    def _(k):
        to = dp_at(k)
        pltpu.make_async_remote_copy(
            val_src(to), val_dst(), val_s, val_r, device_id=(ex, to), device_id_type=MESH
        ).start()

    pltpu.make_async_copy(val_src(me), val_dst(), val_r).start()

    @pl.loop(0, 16)
    def _(r):
        diag[:, pl.ds(pl.multiple_of(r * 64, 64), 64), :] = jnp.zeros((2, 64, 512), BF)

    own_half = (iota((256, 128), 0) // 128) == (iota((256, 128), 1) // 64)

    @pl.loop(0, 8)
    def _(c):
        for load in pair_loads(c):
            load.wait()
        both = dot_nt(
            grad[pl.ds(pl.multiple_of(c * 256, 256), 256), :],
            pout[pl.ds(pl.multiple_of(c * 128, 128), 128), :],
        )
        both = jnp.where(own_half, both, 0.0).astype(BF)
        half, inner = c // 4, lax.rem(c, 4)
        cols = pl.ds(pl.multiple_of(inner * 128, 128), 128)
        for i in range(8):
            for e in range(2):
                rows = pl.ds(pl.multiple_of(i * 128 + inner * 32 + e * 16, 16), 16)
                diag[half, rows, cols] = both[e * 128 + i * 16 : e * 128 + i * 16 + 16, :]

    whole(yrecv, act_r)
    low = iota((64, 128), 1) < 64

    @pl.loop(0, 4)
    def _(q):
        half, inner = q // 2, lax.rem(q, 2)
        cols = pl.ds(pl.multiple_of(inner * 256, 256), 256)
        f = dot(yrecv[half], diag[half, :, cols])
        for h in range(2):
            even, odd = f[:64, h * 128 : h * 128 + 128], f[64:, h * 128 : h * 128 + 128]
            feats[4 * q + 2 * h] = jnp.where(low, even, pltpu.roll(odd, 64, 1)).astype(BF)
            feats[4 * q + 2 * h + 1] = jnp.where(low, pltpu.roll(even, 64, 1), odd).astype(BF)

    def pair(ref, at):
        return ref.at[:, pl.ds(at * 2, 2), :]

    @pl.loop(0, n_dp - 1)
    def _(k):
        to = dp_at(k)
        pltpu.make_async_remote_copy(
            pair(feats, to), pair(train, me), train_s, train_r, device_id=(ex, to), device_id_type=MESH
        ).start()

    pltpu.make_async_copy(pair(feats, me), pair(train, me), train_r).start()

    row, col = iota((256, 256), 0), iota((256, 256), 1)
    swap = ((row // 16 == col % 16) & (row % 16 == col // 16)).astype(BF)
    whole(raw, val_r)

    @pl.loop(0, 8)
    def _(b):
        at = pl.ds(pl.multiple_of(b * 16, 16), 16)
        turned = dot(swap, raw[at].reshape(256, 128)).astype(BF)
        for e in range(16):
            vals[e // 2, at, e % 2 * 128 : e % 2 * 128 + 128] = turned[e * 16 : e * 16 + 16, :]

    whole(train, train_r)
    score = jnp.zeros((64, 128), F32)
    for c in range(8):
        score += dot_nt(jnp.concatenate([train[2 * c], train[2 * c + 1]], axis=1), vals[c])
    part[...] = score

    def two(ref, at):
        return ref.at[pl.ds(at * 2, 2), :]

    @pl.loop(0, n_dp - 1)
    def _(k):
        turn = me % RING_Z * (n_dp // RING_Z) + me // RING_Z
        k = jnp.where(k >= turn, k + 1, k)
        to = lax.rem(k, n_dp // RING_Z) * RING_Z + k // (n_dp // RING_Z)
        pltpu.make_async_remote_copy(
            two(part, to), two(owned, me), part_s, part_r, device_id=(ex, to), device_id_type=MESH
        ).start()

    pltpu.make_async_copy(two(part, me), two(owned, me), part_r).start()
    whole(owned, part_r)

    def folded(value):
        value = value + pltpu.roll(value, 4, 0)
        return value + pltpu.roll(value, 2, 0)

    rows = owned[0:8, :]
    for n in range(1, 8):
        rows += owned[8 * n : 8 * n + 8, :]
    mine[...] = folded(rows)

    @pl.loop(0, n_ex)
    def _(k):
        to = jnp.where(k < 2, 1 - k, k)

        @pl.when(to != ex)
        def _():
            pltpu.make_async_remote_copy(
                mine.at[0:2, :], two(total, ex), own_s, own_r, device_id=(to, me), device_id_type=MESH
            ).start()

    pltpu.make_async_copy(mine.at[0:2, :], two(total, ex), own_r).start()
    whole(total, own_r)
    out_ref[...] = folded(total[0:8, :] + total[8:16, :])[0:2, :]

    whole(yrecv.at[:, :, 0:896], act_s)
    whole(raw.at[0:124], val_s)
    whole(train.at[:, 0:62, :], train_s)
    whole(owned.at[0:62, :], part_s)
    whole(total.at[0:14, :], own_s)


def body(tokens, gates, routes, doc_ids, hidden_grad, proj_in, proj_out, val_features):
    n_dp, n_ex = lax.axis_size("dp"), lax.axis_size("expert")
    entries = proj_out.shape[0] * n_ex * proj_in.shape[1] ** 2
    dma = pltpu.SemaphoreType.DMA
    summed = pl.pallas_call(
        functools.partial(kernel, n_dp, n_ex),
        out_shape=jax.ShapeDtypeStruct((2, 128), F32),
        in_specs=[pl.BlockSpec(memory_space=pltpu.HBM)] * 8,
        out_specs=pl.BlockSpec(memory_space=pltpu.VMEM),
        scratch_shapes=[
            pltpu.VMEM((128, 4096), BF),
            pltpu.VMEM((8, 128), F32),
            pltpu.VMEM((8, 128), jnp.int32),
            pltpu.VMEM((1, 128), jnp.int32),
            pltpu.VMEM((2048, 1536), BF),
            pltpu.VMEM((64, 4096), BF),
            pltpu.VMEM((1024, 1536), BF),
            pltpu.VMEM((128, 128), F32),
            pltpu.VMEM((128, 128), F32),
            pltpu.VMEM((8, 2, 128, 128), BF),
            pltpu.VMEM((2, 128, 1024), BF),
            pltpu.VMEM((2, 1024, 512), BF),
            pltpu.VMEM((16, 64, 128), BF),
            pltpu.VMEM((128, 16, 128), BF),
            pltpu.VMEM((8, 128, 256), BF),
            pltpu.VMEM((16, 64, 128), BF),
            pltpu.VMEM((64, 128), F32),
            pltpu.VMEM((64, 128), F32),
            pltpu.VMEM((16, 128), F32),
            pltpu.VMEM((8, 128), F32),
            dma((5,)),
            dma((2, 8)),
        ]
        + [dma] * 10,
        compiler_params=pltpu.CompilerParams(
            collective_id=0, has_side_effects=True, vmem_limit_bytes=60 << 20
        ),
    )(
        tokens,
        gates.T,
        routes.T,
        doc_ids.reshape(1, -1),
        hidden_grad.reshape(-1, hidden_grad.shape[2]),
        proj_in.T,
        jnp.swapaxes(proj_out, 1, 2).reshape(-1, proj_out.shape[1]),
        val_features,
    )
    return summed * (1.0 / jnp.sqrt(F32(entries)))


def solution(mesh):
    in_specs = (
        P(("expert", "dp"), None),
        P(("expert", "dp"), None),
        P(("expert", "dp"), None),
        P(("expert", "dp")),
        P("expert", "dp", None),
        P(),
        P("expert", None, None),
        P("dp", "expert", None),
    )
    return jax.shard_map(body, mesh=mesh, in_specs=in_specs, out_specs=P("dp", None), check_vma=False)
```
